32 devices in a mesh: dp: 8 (over y, x, core), tensor: 4 (over z).
Axes of the slice: x: 2, y: 2, z: 4, core: 2. Of those that a mesh axis runs over, the one named last changes fastest.
Arguments:
- tokens: bfloat16 [16384, 768], P('dp'), may hold values from -6 to 6
- teacher: bfloat16 [16384, 768], P('dp'), may hold values from -6 to 6
- segment_ids: int32 [32, 512], P('dp'), may hold values from 0 to 7, never falling along the last dimension, each value on 1 to 256 neighbouring positions
- qkv_latent: bfloat16 [2, 768, 3, 768], P(None, 'dp', None, 'tensor'), may hold values from -1.5 to 1.5
- qv_bias: float32 [2, 768], P(None, 'tensor'), may hold values from -3 to 3
- proj_latent: bfloat16 [2, 768, 768], P(None, 'tensor', 'dp'), may hold values from -1.5 to 1.5
- proj_bias: float32 [768], replicated, may hold values from -3 to 3
- up_latent: bfloat16 [2, 768, 3072], P(None, 'dp', 'tensor'), may hold values from -1.5 to 1.5
- up_bias: float32 [3072], P('tensor'), may hold values from -3 to 3
- down_latent: bfloat16 [2, 3072, 768], P(None, 'tensor', 'dp'), may hold values from -1.5 to 1.5
- down_bias: float32 [768], replicated, may hold values from -3 to 3
- norm_gain: float32 [2, 768], replicated, may hold values from 0.5 to 1.5
- norm_shift: float32 [2, 768], replicated, may hold values from -3 to 3
- clip_bounds: float32 [4], replicated, may hold values from 1 to 3, as said below
- binary_scales: float32 [6, 2], replicated, as said below
Outputs:
- block_out: bfloat16 [16384, 768], P('dp')
- input_grad: float32 [16384, 768], P('dp')
- qkv_grad: float32 [2, 768, 3, 768], P(None, 'dp', None, 'tensor')
- qv_bias_grad: float32 [2, 768], P(None, 'tensor')
- proj_grad: float32 [2, 768, 768], P(None, 'tensor', 'dp')
- proj_bias_grad: float32 [768], replicated
- up_grad: float32 [2, 768, 3072], P(None, 'dp', 'tensor')
- up_bias_grad: float32 [3072], P('tensor')
- down_grad: float32 [2, 3072, 768], P(None, 'tensor', 'dp')
- down_bias_grad: float32 [768], replicated
- gain_grad: float32 [2, 768], replicated
- shift_grad: float32 [2, 768], replicated
- clip_grad: float32 [4], replicated
- scale_grad: float32 [6, 2], replicated
The draws below stay inside these ranges and needn't reach their ends.
Inputs may be any that keep to these rules, and one draw needn't show every extreme that they name: `segment_ids`: within each packed sequence the ids never fall and run through 0 to 7; every document has 1 to 256 tokens and some document has exactly 256. `binary_scales`: every scale is positive. `clip_bounds`: every bound is positive.
All inputs are finite; a program needn't handle non-finite values.
Results may differ from the reference program's by a relative error of at most 0.019.
Values may be sent and summed in bfloat16 or wider, within the bound.
A program may use at most 192 MiB of HBM per device.

```python
import math
import jax
import jax.numpy as jnp
import numpy as np
from jax import lax

D = 768
HEADS = 12
HEAD_DIM = 64
FF = 3072
SEQ = 512
DOCS = 8
DOC_MOST = 256
SEQS = 32
TOKENS = 16384
N_DP = 8
N_TENSOR = 4


def draw_binary_scales(key, part):
    base_draw = jax.random.uniform(key, (6, 2), jnp.float32, 0.5, 1.0)
    width_norm = D ** (-0.5)
    factors = jnp.array([1.5 * width_norm, 1.5 * width_norm, width_norm, 3.0 * width_norm, width_norm, 1.5 * FF ** (-0.5)], jnp.float32)
    return base_draw * factors[:, None]


def draw_clip_bounds(key, part):
    unit_draw = jax.random.uniform(jax.random.fold_in(key, 7), (4,), jnp.float32, 0.0, 1.0)
    lower_ends = jnp.array([1.0, 1.0, 1.5, 1.5], jnp.float32)
    upper_ends = jnp.array([2.0, 2.0, 3.0, 3.0], jnp.float32)
    return lower_ends + unit_draw * (upper_ends - lower_ends)


def strengthened(values, stream_key, source, target, shards_of, factor):
    def block_of(axis_at):
        return (jnp.arange(values.shape[axis_at]) // (values.shape[axis_at] // shards_of)).reshape((-1,) + (1,) * (values.ndim - 1 - axis_at))

    first = jax.random.permutation(stream_key, shards_of)[block_of(target)]
    other_side = (block_of(target) + shards_of // 2) % shards_of
    return jnp.where((block_of(source) == first) | (block_of(source) == other_side), factor * values, values)


def level_of(own_key, extent, cuts, smallest, high):
    factor_of = 1.0
    for axis_at, parts in cuts:
        steps = jax.random.uniform(jax.random.fold_in(jax.random.fold_in(own_key, 6), axis_at), (parts,), jnp.float32, smallest / len(cuts), high / len(cuts))
        factor_of = factor_of * jnp.repeat(jnp.exp(steps), extent[axis_at] // parts).reshape((-1,) + (1,) * (len(extent) - 1 - axis_at))
    return factor_of


def length_profile(amount, total, reach, lean):
    portions = [(1 << 20) // math.isqrt(grade ** lean) + 1 for grade in range(2, amount + 1)]
    spare, holding = total - reach - (amount - 1), [1] * (amount - 1)
    while spare > 0:
        free = [i for i in range(amount - 1) if holding[i] < reach]
        mass, left = sum([portions[i] for i in free]), spare
        for i in free:
            more = min(reach - holding[i], max(1, left * portions[i] // mass), spare)
            holding[i] = holding[i] + more
            spare = spare - more
    return np.array([reach] + holding)


def uneven(rng, number_of, total, limit, skew):
    if number_of == 2:
        one = jax.random.randint(rng, (), max(1, total - limit), min(limit, total - 1) + 1)
        return jnp.stack([one, total - one])
    lengths = jnp.asarray(length_profile(number_of, total, limit, skew), jnp.int32)
    pairs = (number_of - 1) // 2
    giver, receiver = lengths[1:1 + 2 * pairs:2], lengths[2:2 + 2 * pairs:2]
    slack = jnp.minimum(giver - 1, limit - receiver)
    shifted = jax.random.randint(jax.random.fold_in(rng, 1), (pairs,), 0, 1 << 20) % (slack + 1)
    lengths = lengths.at[1:1 + 2 * pairs:2].set(giver - shifted).at[2:2 + 2 * pairs:2].set(receiver + shifted)
    return lengths[jax.random.permutation(jax.random.fold_in(rng, 2), number_of)]


def bell_draw(rng, extent, width, bound, split=(), kind=jnp.bfloat16):
    level = level_of(rng, extent, split, -0.22, 0.18) if split else 1.0
    values = jax.random.normal(rng, extent, jnp.float32) * width * level
    return jnp.minimum(jnp.maximum(values, -bound), bound).astype(kind)


def noise_with(stream_key, dims, scale, bound, pieces, heavy, kind=jnp.bfloat16):
    values = scale * jax.random.normal(stream_key, dims, jnp.float32)
    if pieces:
        values = values * level_of(stream_key, dims, pieces, -0.22, 0.18)
    return jnp.clip(strengthened(values, jax.random.fold_in(stream_key, 3), *heavy), -bound, bound).astype(kind)


def setup_inputs(seed: int = 0) -> dict:
    key_list = jax.random.split(jax.random.key(seed), 16)
    tokens = noise_with(key_list[0], (TOKENS, D), 1.0, 6.0, ((0, 8),), (0, 1, 8, 2.0))
    teacher = noise_with(key_list[1], (TOKENS, D), 1.0, 6.0, ((0, 8),), (0, 1, 8, 2.0))
    segment_ids = jax.vmap(lambda own: jnp.searchsorted(jnp.cumsum(uneven(own, DOCS, SEQ, DOC_MOST, 2)), jnp.arange(SEQ), side="right"))(jax.random.split(key_list[2], SEQS)).reshape((SEQS, SEQ)).astype(jnp.int32)
    qkv_latent = jnp.clip(jax.random.uniform(key_list[3], (2, D, 3, D), jnp.float32, -1.5, 1.5) * level_of(key_list[3], (2, D, 3, D), ((1, 8), (3, 4)), -0.4, 0.0), -1.5, 1.5).astype(jnp.bfloat16)
    qv_bias = bell_draw(key_list[4], (2, D), 0.5, 3.0, ((1, 4),), jnp.float32)
    proj_latent = jnp.clip(jax.random.uniform(key_list[5], (2, D, D), jnp.float32, -1.5, 1.5) * level_of(key_list[5], (2, D, D), ((1, 4), (2, 8)), -0.4, 0.0), -1.5, 1.5).astype(jnp.bfloat16)
    proj_bias = bell_draw(key_list[6], (D,), 0.5, 3.0, (), jnp.float32)
    up_latent = jnp.clip(jax.random.uniform(key_list[7], (2, D, FF), jnp.float32, -1.5, 1.5) * level_of(key_list[7], (2, D, FF), ((1, 8), (2, 4)), -0.4, 0.0), -1.5, 1.5).astype(jnp.bfloat16)
    up_bias = bell_draw(key_list[8], (FF,), 0.5, 3.0, ((0, 4),), jnp.float32)
    down_latent = jnp.clip(jax.random.uniform(key_list[9], (2, FF, D), jnp.float32, -1.5, 1.5) * level_of(key_list[9], (2, FF, D), ((1, 4), (2, 8)), -0.4, 0.0), -1.5, 1.5).astype(jnp.bfloat16)
    down_bias = bell_draw(key_list[10], (D,), 0.5, 3.0, (), jnp.float32)
    norm_gain = jnp.clip(1.0 + 0.1 * jax.random.normal(key_list[11], (2, D), jnp.float32), 0.5, 1.5)
    norm_shift = bell_draw(key_list[12], (2, D), 0.5, 3.0, (), jnp.float32)
    clip_bounds = draw_clip_bounds(jax.random.fold_in(key_list[15], 71), 0)
    binary_scales = draw_binary_scales(jax.random.fold_in(key_list[15], 71), 0)
    return dict(tokens=tokens, teacher=teacher, segment_ids=segment_ids, qkv_latent=qkv_latent, qv_bias=qv_bias, proj_latent=proj_latent, proj_bias=proj_bias, up_latent=up_latent, up_bias=up_bias, down_latent=down_latent, down_bias=down_bias, norm_gain=norm_gain, norm_shift=norm_shift, clip_bounds=clip_bounds, binary_scales=binary_scales)


@jax.custom_vjp
def low(v):
    return lax.optimization_barrier(v.astype(jnp.bfloat16)).astype(jnp.float32)

@jax.custom_vjp
def low_back(v):
    return v

def low_keep(v):
    return (low(v), None)

def low_pass(kept, grad):
    return (grad,)

def back_keep(v):
    return (v, None)

def back_low(kept, grad):
    return (low(grad),)
low.defvjp(low_keep, low_pass)
low_back.defvjp(back_keep, back_low)
highest = lax.Precision.HIGHEST

def clip_to(values, clip_at):
    return clip_at * jnp.tanh(values / clip_at)

def binarize(latent, held_latent, scale_first, scale_second):
    moving = jnp.where(jnp.abs(latent) < 1.0, latent, jnp.sign(latent))
    held_part = jnp.where(jnp.abs(held_latent) < 1.0, held_latent, jnp.sign(held_latent))
    sign_vals = moving - held_part + jnp.sign(held_latent)
    return low(scale_first * sign_vals[0] + scale_second * sign_vals[1])

def layer_norm(values, gain, shift):
    centre = values - lax.optimization_barrier(jnp.mean(values, axis=-1, keepdims=True))
    spread = lax.optimization_barrier(jnp.mean(centre * centre, axis=-1, keepdims=True))
    return centre * lax.rsqrt(spread + 1e-12) * gain + shift

def forward(tokens, qkv_latent, qv_bias, proj_latent, proj_bias, up_latent, up_bias, down_latent, down_bias, norm_gain, norm_shift, clip_bounds, binary_scales, held_latents, same_doc):
    groups = N_TENSOR
    group_cols = D // groups
    unit_cols = FF // groups
    heads_group = HEADS // groups
    tok_rows = tokens.shape[0]
    seq_count = tok_rows // SEQ
    qkv_held, proj_held, up_held, down_held = held_latents
    w_qkv = binarize(qkv_latent, qkv_held, binary_scales[0:3, 0][:, None], binary_scales[0:3, 1][:, None])
    w_proj = binarize(proj_latent, proj_held, binary_scales[3, 0], binary_scales[3, 1])
    w_up = binarize(up_latent, up_held, binary_scales[4, 0], binary_scales[4, 1])
    w_down = binarize(down_latent, down_held, binary_scales[5, 0], binary_scales[5, 1])
    act_one = low(clip_to(tokens, clip_bounds[0]))
    spread_one = low_back(jnp.broadcast_to(act_one, (groups, tok_rows, D)))
    qkv_grouped = w_qkv.reshape(D, 3, groups, group_cols)
    qkv_all = jnp.einsum('grd,dmgc->gmrc', spread_one, qkv_grouped, precision=highest)
    bias_rows = jnp.stack([qv_bias[0], jnp.zeros_like(qv_bias[0]), qv_bias[1]])
    bias_rows = bias_rows.reshape(3, groups, group_cols).transpose(1, 0, 2)[:, :, None, :]
    qkv_all = low_back(low(qkv_all + bias_rows))
    split_shape = (groups, seq_count, SEQ, heads_group, HEAD_DIM)
    queries = qkv_all[:, 0].reshape(split_shape)
    key_heads = qkv_all[:, 1].reshape(split_shape)
    values = qkv_all[:, 2].reshape(split_shape)
    scores = jnp.einsum('gnqhe,gnkhe->gnhqk', queries, key_heads, precision=highest) * HEAD_DIM ** (-0.5)
    scores = jnp.where(same_doc[None, :, None], scores, -1000000000.0)
    scores = low_back(scores)
    prob_rows = jax.nn.softmax(scores, axis=-1)
    prob_low = low(prob_rows)
    context = jnp.einsum('gnhqk,gnkhe->gnqhe', prob_low, values, precision=highest).reshape(groups, tok_rows, group_cols)
    context = low_back(context)
    act_two = low(clip_to(context, clip_bounds[1]))
    attn_parts = jnp.einsum('grc,gcd->grd', act_two, w_proj.reshape(groups, group_cols, D), precision=highest)
    attention = low_back(lax.optimization_barrier(jnp.sum(low(attn_parts), axis=0))) + proj_bias
    h_one = layer_norm(tokens + attention, norm_gain[0], norm_shift[0])
    act_three = low(clip_to(h_one, clip_bounds[2]))
    spread_three = low_back(jnp.broadcast_to(act_three, (groups, tok_rows, D)))
    hidden = jnp.einsum('grd,dgu->gru', spread_three, w_up.reshape(D, groups, unit_cols), precision=highest)
    hidden = low_back(hidden + up_bias.reshape(groups, 1, unit_cols))
    act_four = low(clip_to(jax.nn.gelu(hidden, approximate=False), clip_bounds[3]))
    ffn_parts = jnp.einsum('gru,gud->grd', act_four, w_down.reshape(groups, unit_cols, D), precision=highest)
    feed_out = low_back(lax.optimization_barrier(jnp.sum(low(ffn_parts), axis=0))) + down_bias
    return layer_norm(h_one + feed_out, norm_gain[1], norm_shift[1])

def reference(tokens, teacher, segment_ids, qkv_latent, qv_bias, proj_latent, proj_bias, up_latent, up_bias, down_latent, down_bias, norm_gain, norm_shift, clip_bounds, binary_scales):
    params = tuple((p.astype(jnp.float32) for p in (qkv_latent, qv_bias, proj_latent, proj_bias, up_latent, up_bias, down_latent, down_bias, norm_gain, norm_shift, clip_bounds, binary_scales)))
    held_latents = (params[0], params[2], params[4], params[6])
    blocks = N_DP
    block_rows = tokens.shape[0] // blocks
    token_blocks = tokens.reshape(blocks, block_rows, D)
    teacher_blocks = teacher.reshape(blocks, block_rows, D)
    segment_blocks = segment_ids.reshape(blocks, block_rows // SEQ, SEQ)

    def one_block(totals, inputs):
        block_tokens, block_teacher, block_segments = inputs
        same_doc = block_segments[:, :, None] == block_segments[:, None, :]

        def block_fn(x_block, *param_list):
            return forward(x_block, *param_list, held_latents, same_doc)
        output, pull_back = jax.vjp(block_fn, block_tokens.astype(jnp.float32), *params)
        gradients = pull_back(output - block_teacher.astype(jnp.float32))
        totals = tuple((t + g for t, g in zip(totals, gradients[1:])))
        return (totals, (output.astype(jnp.bfloat16), gradients[0]))
    zero_sums = tuple((jnp.zeros_like(p) for p in params))
    totals, (outputs, input_grads) = lax.scan(one_block, zero_sums, (token_blocks, teacher_blocks, segment_blocks))
    return (outputs.reshape(-1, D), input_grads.reshape(-1, D), totals[0], totals[1], totals[2], totals[3], totals[4], totals[5], totals[6], totals[7], totals[8], totals[9], totals[10], totals[11])
```

```python
import jax
import jax.numpy as jnp
from jax import lax
from jax.sharding import PartitionSpec as P

HEAD_DIM = 64
F32 = jnp.float32
LOW = jnp.bfloat16


def dot_nn(a, b):
    return lax.dot_general(a, b, (((1,), (0,)), ((), ())), preferred_element_type=F32)


def dot_nt(a, b):
    return lax.dot_general(a, b, (((1,), (1,)), ((), ())), preferred_element_type=F32)


def dot_tn(a, b):
    return lax.dot_general(a, b, (((0,), (0,)), ((), ())), preferred_element_type=F32)


def squash(values, clip_at):
    ratio = values / clip_at
    bent = jnp.tanh(ratio)
    return (clip_at * bent, bent, ratio)


def squash_back(gradient, bent, ratio):
    slope = 1.0 - bent * bent
    return (gradient * slope, jnp.sum(gradient * (bent - ratio * slope)))


def norm_parts(values, gain, shift):
    centre = values - jnp.mean(values, axis=-1, keepdims=True)
    scale_inv = lax.rsqrt(jnp.mean(centre * centre, axis=-1, keepdims=True) + 1e-12)
    normed = centre * scale_inv
    return (normed * gain + shift, normed, scale_inv)


def norm_back(gradient, normed, scale_inv, gain):
    scaled = gradient * gain
    return scale_inv * (
        scaled
        - jnp.mean(scaled, axis=-1, keepdims=True)
        - normed * jnp.mean(scaled * normed, axis=-1, keepdims=True)
    )


def exact_gelu(values):
    return jax.nn.gelu(values, approximate=False)


def shards(
    tokens,
    teacher,
    segment_ids,
    qkv_latent,
    qv_bias,
    proj_latent,
    proj_bias,
    up_latent,
    up_bias,
    down_latent,
    down_bias,
    norm_gain,
    norm_shift,
    clip_bounds,
    binary_scales,
):
    groups = lax.axis_size("tensor")
    parts = lax.axis_size("dp")
    group = lax.axis_index("tensor")
    seqs = segment_ids.shape[0] // groups
    length = segment_ids.shape[1]
    rows = seqs * length
    model = tokens.shape[1]
    own_rows = qkv_latent.shape[1]
    head_cols = qkv_latent.shape[3]
    units = up_latent.shape[2]
    heads = head_cols // HEAD_DIM

    tokens = lax.dynamic_slice_in_dim(tokens, group * rows, rows, 0)
    teacher = lax.dynamic_slice_in_dim(teacher, group * rows, rows, 0)
    segment_ids = lax.dynamic_slice_in_dim(segment_ids, group * seqs, seqs, 0)

    latents = jnp.concatenate(
        [
            qkv_latent.reshape(2, own_rows, 3 * head_cols),
            proj_latent.transpose(0, 2, 1),
            up_latent,
            down_latent.transpose(0, 2, 1),
        ],
        axis=2,
    )
    widths = [head_cols] * 4 + [units] * 2
    scale_cols = jnp.concatenate(
        [jnp.broadcast_to(binary_scales[m][:, None], (2, w)) for m, w in enumerate(widths)], axis=1
    )
    signs = jnp.sign(latents).astype(F32)
    w_own = (scale_cols[0] * signs[0] + scale_cols[1] * signs[1]).astype(LOW)
    w_all = lax.all_gather(w_own, ("tensor", "dp"), axis=0, tiled=False)
    w_all = w_all.reshape(groups, model, 4 * head_cols + 2 * units)
    bias_all = lax.all_gather(
        jnp.concatenate([qv_bias[0], qv_bias[1], up_bias]), "tensor", axis=0, tiled=False
    )
    edge = 3 * head_cols

    inputs = tokens.astype(F32)
    act_one_full, bent_zero, ratio_zero = squash(inputs, clip_bounds[0])
    act_one = act_one_full.astype(LOW)
    same_doc = (segment_ids[:, :, None] == segment_ids[:, None, :])[:, None]
    factor = HEAD_DIM ** (-0.5)

    attention = jnp.zeros((rows, model), F32)
    kept = []
    for g in range(groups):
        w_qkv = w_all[g, :, :edge]
        bias = jnp.concatenate(
            [
                bias_all[g, :head_cols],
                jnp.zeros((head_cols,), F32),
                bias_all[g, head_cols : 2 * head_cols],
            ]
        )
        qkv = (dot_nn(act_one, w_qkv) + bias).astype(LOW).reshape(seqs, length, 3, heads, HEAD_DIM)
        q, k, v = qkv[:, :, 0], qkv[:, :, 1], qkv[:, :, 2]
        scores = jnp.einsum("nqhe,nkhe->nhqk", q, k, preferred_element_type=F32) * factor
        scores = jnp.where(same_doc, scores, -1000000000.0)
        top = jnp.max(scores, axis=-1, keepdims=True)
        terms = jnp.exp(scores - top)
        total = jnp.sum(terms, axis=-1, keepdims=True)
        probs = (terms / total).astype(LOW)
        context = jnp.einsum("nhqk,nkhe->nqhe", probs, v, preferred_element_type=F32).reshape(
            rows, head_cols
        )
        act_full, bent_one, ratio_one = squash(context, clip_bounds[1])
        act_two = act_full.astype(LOW)
        attention += dot_nt(act_two, w_all[g, :, edge : edge + head_cols]).astype(LOW).astype(F32)
        kept.append((q, k, v, probs, act_two, bent_one, ratio_one))
    h_one, normed_one, inv_one = norm_parts(inputs + (attention + proj_bias), norm_gain[0], norm_shift[0])
    act_three_full, bent_two, ratio_two = squash(h_one, clip_bounds[2])
    act_three = act_three_full.astype(LOW)

    feed = jnp.zeros((rows, model), F32)
    start_up = 4 * head_cols
    start_down = start_up + units
    kept_ffn = []
    for g in range(groups):
        hidden = dot_nn(act_three, w_all[g, :, start_up:start_down]) + bias_all[g, 2 * head_cols :]
        activated, gelu_back = jax.vjp(exact_gelu, hidden)
        act_full, bent_three, ratio_three = squash(activated, clip_bounds[3])
        act_four = act_full.astype(LOW)
        feed += dot_nt(act_four, w_all[g, :, start_down:]).astype(LOW).astype(F32)
        kept_ffn.append((act_four, gelu_back, bent_three, ratio_three))
    y_full, normed_two, inv_two = norm_parts(h_one + (feed + down_bias), norm_gain[1], norm_shift[1])
    block_out = lax.all_gather(y_full.astype(LOW), "tensor", axis=0, tiled=True)

    out_grad = y_full - teacher.astype(F32)
    gain_two = jnp.sum(out_grad * normed_two, axis=0)
    shift_two = jnp.sum(out_grad, axis=0)
    grad_two = norm_back(out_grad, normed_two, inv_two, norm_gain[1])
    down_bias_part = jnp.sum(grad_two, axis=0)
    grad_two_low = grad_two.astype(LOW)
    grads = [[] for _ in range(groups)]
    up_bias_part = []
    clip_three = 0.0
    grad_three = jnp.zeros((rows, model), F32)
    g_down, g_up = [], []
    for g in range(groups):
        act_four, gelu_back, bent_three, ratio_three = kept_ffn[g]
        g_down.append(dot_tn(grad_two_low, act_four).astype(LOW))
        grad_four = dot_nn(grad_two_low, w_all[g, :, start_down:])
        grad_act, clip_part = squash_back(grad_four, bent_three, ratio_three)
        clip_three += clip_part
        grad_hidden = gelu_back(grad_act)[0].astype(LOW)
        up_bias_part.append(jnp.sum(grad_hidden.astype(F32), axis=0))
        g_up.append(dot_tn(act_three, grad_hidden).astype(LOW))
        grad_three += dot_nt(grad_hidden, w_all[g, :, start_up:start_down]).astype(LOW).astype(F32)
    grad_three_in, clip_two = squash_back(grad_three, bent_two, ratio_two)
    grad_h = grad_two + grad_three_in
    gain_one = jnp.sum(grad_h * normed_one, axis=0)
    shift_one = jnp.sum(grad_h, axis=0)
    grad_one = norm_back(grad_h, normed_one, inv_one, norm_gain[0])
    proj_bias_part = jnp.sum(grad_one, axis=0)
    grad_one_low = grad_one.astype(LOW)

    clip_one = 0.0
    grad_act_one = jnp.zeros((rows, model), F32)
    g_att = []
    q_bias_part, v_bias_part = [], []
    for g in range(groups):
        q, k, v, probs, act_two, bent_one, ratio_one = kept[g]
        w_o = w_all[g, :, edge : edge + head_cols]
        g_proj = dot_tn(grad_one_low, act_two).astype(LOW)
        grad_ctx, clip_part = squash_back(dot_nn(grad_one_low, w_o), bent_one, ratio_one)
        clip_one += clip_part
        grad_ctx = grad_ctx.astype(LOW).reshape(seqs, length, heads, HEAD_DIM)
        grad_v = jnp.einsum("nhqk,nqhe->nkhe", probs, grad_ctx, preferred_element_type=F32)
        grad_probs = jnp.einsum("nqhe,nkhe->nhqk", grad_ctx, v, preferred_element_type=F32)
        probs_wide = probs.astype(F32)
        grad_scores = (
            probs_wide * (grad_probs - jnp.sum(probs_wide * grad_probs, axis=-1, keepdims=True))
        ).astype(LOW)
        grad_q = jnp.einsum("nhqk,nkhe->nqhe", grad_scores, k, preferred_element_type=F32) * factor
        grad_k = jnp.einsum("nhqk,nqhe->nkhe", grad_scores, q, preferred_element_type=F32) * factor
        grad_qkv = jnp.stack([grad_q, grad_k, grad_v], axis=2).astype(LOW).reshape(rows, edge)
        sums = jnp.sum(grad_qkv.astype(F32), axis=0)
        q_bias_part.append(sums[:head_cols])
        v_bias_part.append(sums[2 * head_cols :])
        g_qkv = dot_tn(act_one, grad_qkv).astype(LOW)
        g_att.append(jnp.concatenate([g_qkv, g_proj], axis=1))
        grad_act_one += dot_nt(grad_qkv, w_all[g, :, :edge]).astype(LOW).astype(F32)
    grad_inputs, clip_zero = squash_back(grad_act_one, bent_zero, ratio_zero)
    input_grad = lax.all_gather(
        (grad_one + grad_inputs).astype(LOW), "tensor", axis=0, tiled=True
    ).astype(F32)

    g_all = jnp.stack(
        [jnp.concatenate([g_att[g], g_up[g], g_down[g]], axis=1) for g in range(groups)]
    ).reshape(groups * parts, own_rows, 4 * head_cols + 2 * units)
    g_own = lax.psum_scatter(
        g_all, ("tensor", "dp"), scatter_dimension=0, tiled=False
    ).astype(F32)

    keep = jnp.abs(latents) < 1.0
    terms = jnp.where(keep, g_own[None] * scale_cols[:, None], 0.0)
    col_sums = jnp.sum(g_own[None] * signs, axis=1)
    ends = [0]
    for w in widths:
        ends.append(ends[-1] + w)
    scale_parts = jnp.stack([jnp.sum(col_sums[:, a:b], axis=1) for a, b in zip(ends[:-1], ends[1:])])

    clip_parts = jnp.stack([clip_zero, clip_one, clip_two, clip_three])
    small = jnp.concatenate(
        [
            jnp.concatenate(q_bias_part),
            jnp.concatenate(v_bias_part),
            jnp.concatenate(up_bias_part),
            proj_bias_part,
            down_bias_part,
            gain_one,
            gain_two,
            shift_one,
            shift_two,
            clip_parts,
            scale_parts.reshape(-1),
        ]
    )
    small = lax.psum(small, ("dp", "tensor"))
    pos = 0

    def take(n):
        nonlocal pos
        out = small[pos : pos + n]
        pos += n
        return out

    q_bias = lax.dynamic_slice_in_dim(take(groups * head_cols), group * head_cols, head_cols, 0)
    v_bias = lax.dynamic_slice_in_dim(take(groups * head_cols), group * head_cols, head_cols, 0)
    up_bias_grad = lax.dynamic_slice_in_dim(take(groups * units), group * units, units, 0)
    proj_bias_grad = take(model)
    down_bias_grad = take(model)
    gain_grad = take(2 * model).reshape(2, model)
    shift_grad = take(2 * model).reshape(2, model)
    clip_grad = take(4)
    scale_grad = take(12).reshape(6, 2)
    return (
        block_out,
        input_grad,
        terms[:, :, :edge].reshape(2, own_rows, 3, head_cols),
        jnp.stack([q_bias, v_bias]),
        terms[:, :, edge : edge + head_cols].transpose(0, 2, 1),
        proj_bias_grad,
        terms[:, :, start_up:start_down],
        up_bias_grad,
        terms[:, :, start_down:].transpose(0, 2, 1),
        down_bias_grad,
        gain_grad,
        shift_grad,
        clip_grad,
        scale_grad,
    )


def solution(mesh):
    return jax.shard_map(
        shards,
        mesh=mesh,
        in_specs=(
            P("dp", None),
            P("dp", None),
            P("dp", None),
            P(None, "dp", None, "tensor"),
            P(None, "tensor"),
            P(None, "tensor", "dp"),
            P(),
            P(None, "dp", "tensor"),
            P("tensor"),
            P(None, "tensor", "dp"),
            P(),
            P(),
            P(),
            P(),
            P(),
        ),
        out_specs=(
            P("dp", None),
            P("dp", None),
            P(None, "dp", None, "tensor"),
            P(None, "tensor"),
            P(None, "tensor", "dp"),
            P(),
            P(None, "dp", "tensor"),
            P("tensor"),
            P(None, "tensor", "dp"),
            P(),
            P(),
            P(),
            P(),
            P(),
        ),
        check_vma=False,
    )
```

```python
import jax
import jax.numpy as jnp
from jax import lax
from jax.experimental import pallas as pl
from jax.experimental.pallas import tpu as pltpu
from jax.sharding import PartitionSpec as P

HEAD_DIM = 64
F32 = jnp.float32
LOW = jnp.bfloat16


def dot_nn(a, b):
    return lax.dot_general(a, b, (((1,), (0,)), ((), ())), preferred_element_type=F32)


def dot_nt(a, b):
    return lax.dot_general(a, b, (((1,), (1,)), ((), ())), preferred_element_type=F32)


def dot_tn(a, b):
    return lax.dot_general(a, b, (((0,), (0,)), ((), ())), preferred_element_type=F32)


def dot_tt(a, b):
    return lax.dot_general(a, b, (((0,), (1,)), ((), ())), preferred_element_type=F32)


MESH = pl.DeviceIdType.MESH
NO_MATCH = -1000000000.0
HALVES = (pl.ds(0, 2), pl.ds(2, 2))


class Place:
    def __init__(self):
        at = lax.axis_index("dp")
        self.t = lax.axis_index("tensor")
        self.core = lax.rem(at, 2)
        self.j = lax.div(at, 2)
        x = lax.rem(self.j, 2)
        y = lax.div(self.j, 2)
        self.jx = 2 * y + (1 - x)
        self.jy = 2 * (1 - y) + x
        self.jd = 2 * (1 - y) + (1 - x)
        self.p_core = {"dp": 2 * self.j + (1 - self.core)}
        self.p_x = {"dp": 2 * self.jx + self.core}
        self.p_y = {"dp": 2 * self.jy + self.core}

    def z(self, k):
        return lax.rem(self.t + k, 4)

    def p_z(self, k):
        return {"tensor": self.z(k)}


def remote(src, dst, send, recv, device):
    return pltpu.make_async_remote_copy(src, dst, send, recv, device_id=device, device_id_type=MESH)


class Gather:
    def __init__(self, w, send, recv, place):
        self.w, self.send, self.recv, self.pc = w, send, recv, place

    def cp(self, c, i, region, device):
        ref = self.w.at[region]
        return remote(ref, ref, self.send.at[c, i], self.recv.at[c, i], device)

    def z_start(self, c):
        pc = self.pc
        for k in (1, 2, 3):
            self.cp(c, k - 1, (c, pc.t, pc.j, pc.core), pc.p_z(k)).start()

    def z_wait_xy_start(self, c):
        pc = self.pc
        for k in (1, 2, 3):
            self.cp(c, k - 1, (c, pc.z(4 - k), pc.j, pc.core), pc.p_z(k)).wait_recv()
        a, b = HALVES
        self.cp(c, 3, (c, a, pc.j, pc.core), pc.p_x).start()
        self.cp(c, 4, (c, b, pc.j, pc.core), pc.p_y).start()
        self.cp(c, 5, (c, a, pc.j, pc.core), pc.p_y).start()
        self.cp(c, 7, (c, b, pc.j, pc.core), pc.p_x).start()
        self.cp(c, 9, (c, a, pc.j, pc.core), pc.p_core).start()
        self.cp(c, 10, (c, b, pc.j, pc.core), pc.p_core).start()

    def relay(self, c):
        pc = self.pc
        a, b = HALVES
        self.cp(c, 3, (c, a, pc.jx, pc.core), pc.p_x).wait_recv()
        self.cp(c, 6, (c, a, pc.jx, pc.core), pc.p_y).start()
        self.cp(c, 11, (c, a, pc.jx, pc.core), pc.p_core).start()
        self.cp(c, 4, (c, b, pc.jy, pc.core), pc.p_y).wait_recv()
        self.cp(c, 8, (c, b, pc.jy, pc.core), pc.p_x).start()
        self.cp(c, 12, (c, b, pc.jy, pc.core), pc.p_core).start()

    def finish(self, c):
        pc = self.pc
        a, b = HALVES
        other = 1 - pc.core
        rest = ((5, a, pc.jy, pc.p_y), (7, b, pc.jx, pc.p_x), (6, a, pc.jd, pc.p_y), (8, b, pc.jd, pc.p_x))
        for n, (i, half, j, device) in enumerate(rest):
            self.cp(c, i, (c, half, j, pc.core), device).wait_recv()
            self.cp(c, 13 + n, (c, half, j, pc.core), pc.p_core).start()
        order = ((a, pc.j), (b, pc.j), (a, pc.jx), (b, pc.jy), (a, pc.jy), (b, pc.jx), (a, pc.jd), (b, pc.jd))
        for n, (half, j) in enumerate(order):
            self.cp(c, 9 + n, (c, half, j, other), pc.p_core).wait_recv()

    def sent(self, c):
        pc = self.pc
        for i in range(3):
            self.cp(c, i, (c, pc.t, pc.j, pc.core), pc.p_z(1)).wait_send()
        for i in range(3, 17):
            self.cp(c, i, (c, HALVES[0], pc.j, pc.core), pc.p_core).wait_send()


def add_to(dst, src, n):
    def step(i, _):
        at = (lax.div(i, 3), pl.ds(pl.multiple_of(lax.rem(i, 3) * 32, 32), 32))
        dst[at] = (dst[at].astype(F32) + src[at].astype(F32)).astype(LOW)
        return 0

    lax.fori_loop(0, 3 * n, step, 0)


class Scatter:
    def __init__(self, g, l_core, l_two, l_one, l_z, send, recv, credit, place):
        self.g, self.l_core, self.l_two, self.l_one, self.l_z = g, l_core, l_two, l_one, l_z
        self.send, self.recv, self.credit, self.pc = send, recv, credit, place

    def core_cp(self, c, h):
        pc = self.pc
        return remote(
            self.g.at[c, HALVES[h], :, 1 - pc.core],
            self.l_core.at[c % 2, HALVES[h]],
            self.send.at[c, h],
            self.recv.at[c, h],
            pc.p_core,
        )

    def core_start(self, c):
        if c == 0:
            pl.semaphore_wait(self.credit, 1)
        for h in (0, 1):
            self.core_cp(c, h).start()

    def first_peers(self, h):
        pc = self.pc
        return (pc.p_y, pc.jy, pc.jx) if h == 0 else (pc.p_x, pc.jx, pc.jy)

    def two_cp(self, c, h, n):
        pc = self.pc
        device, near, _ = self.first_peers(h)
        j = near if n == 0 else pc.jd
        return remote(
            self.g.at[c, HALVES[h], j, pc.core],
            self.l_two.at[c, h, n],
            self.send.at[c, 2 + 2 * h + n],
            self.recv.at[c, 2 + 2 * h + n],
            device,
        )

    def one_cp(self, c, h):
        pc = self.pc
        device, j = (pc.p_x, pc.jx) if h == 0 else (pc.p_y, pc.jy)
        return remote(
            self.g.at[c, HALVES[h], j, pc.core],
            self.l_one.at[c, h],
            self.send.at[c, 6 + h],
            self.recv.at[c, 6 + h],
            device,
        )

    def z_cp(self, c, k):
        pc = self.pc
        return remote(
            self.g.at[c, pc.z(k), pc.j, pc.core],
            self.l_z.at[c, k - 1],
            self.send.at[c, 7 + k],
            self.recv.at[c, 7 + k],
            pc.p_z(k),
        )

    def core_fin(self, c):
        pc = self.pc
        for h in (0, 1):
            self.core_cp(c, h).wait_recv()
            for j in (pc.jd, self.first_peers(h)[1]):
                for n in (0, 1):
                    add_to(self.g.at[c, pl.ds(2 * h + n, 1), j, pc.core], self.l_core.at[c % 2, pl.ds(2 * h + n, 1), j], 1)
            self.two_cp(c, h, 1).start()
            self.two_cp(c, h, 0).start()
        for h in (0, 1):
            for j in (pc.j, self.first_peers(h)[2]):
                for n in (0, 1):
                    add_to(self.g.at[c, pl.ds(2 * h + n, 1), j, pc.core], self.l_core.at[c % 2, pl.ds(2 * h + n, 1), j], 1)
        if c == 2:
            pl.semaphore_signal(self.credit, inc=1, device_id=pc.p_core, device_id_type=MESH)

    def two_fin(self, c):
        pc = self.pc
        for h in (0, 1):
            self.two_cp(c, h, 1).wait_recv()
            add_to(self.g.at[c, HALVES[h], self.first_peers(h)[2], pc.core], self.l_two.at[c, h, 1], 2)
            self.one_cp(c, h).start()
        for h in (0, 1):
            self.two_cp(c, h, 0).wait_recv()
            add_to(self.g.at[c, HALVES[h], pc.j, pc.core], self.l_two.at[c, h, 0], 2)

    def one_fin(self, c):
        pc = self.pc
        for h in (0, 1):
            self.one_cp(c, h).wait_recv()
            add_to(self.g.at[c, HALVES[h], pc.j, pc.core], self.l_one.at[c, h], 2)
        for k in (2, 1, 3):
            self.z_cp(c, k).start()

    def z_wait(self, c):
        for k in (1, 2, 3):
            self.z_cp(c, k).wait_recv()

    def sent(self, c):
        for h in (0, 1):
            self.core_cp(c, h).wait_send()
            self.two_cp(c, h, 0).wait_send()
            self.two_cp(c, h, 1).wait_send()
            self.one_cp(c, h).wait_send()
        for k in (1, 2, 3):
            self.z_cp(c, k).wait_send()


class Line:
    def __init__(self, own, out, send, recv, local, place):
        self.own, self.out, self.send, self.recv, self.local, self.pc = own, out, send, recv, local, place

    def cp(self, way, k, receive=False):
        t = self.pc.t
        step = 1 if way == 0 else -1
        if receive:
            source = t - step * k
        else:
            source = t - step * (k - 1)
        source = jnp.clip(source, 0, 3)
        dst = self.out.at[source]
        src = self.own if (k == 1 and not receive) else dst
        return remote(src, dst, self.send.at[way, k - 1], self.recv.at[way, k - 1], self.pc.p_z(1 if way == 0 else 3))

    def sends(self, way, k):
        t = self.pc.t
        return (t >= k - 1) & (t < 3) if way == 0 else (t <= 4 - k) & (t > 0)

    def receives(self, way, k):
        t = self.pc.t
        return t >= k if way == 0 else t <= 3 - k

    def start(self):
        pltpu.make_async_copy(self.own, self.out.at[self.pc.t], self.local).start()
        for way in (0, 1):

            @pl.when(self.sends(way, 1))
            def _():
                self.cp(way, 1).start()

    def step(self, k):
        for way in (0, 1):

            @pl.when(self.receives(way, k))
            def _():
                self.cp(way, k, receive=True).wait_recv()

            if k < 3:

                @pl.when(self.sends(way, k + 1))
                def _():
                    self.cp(way, k + 1).start()

    def sent(self):
        pltpu.make_async_copy(self.own, self.out.at[self.pc.t], self.local).wait()
        for way in (0, 1):
            for k in (1, 2, 3):

                @pl.when(self.sends(way, k))
                def _():
                    self.cp(way, k).wait_send()


class SmallSum:
    def __init__(self, held, landed, four, send, recv, place):
        self.held, self.landed, self.four, self.send, self.recv, self.pc = held, landed, four, send, recv, place

    def run(self):
        pc = self.pc
        for n, device in enumerate((pc.p_core, pc.p_x, pc.p_y)):
            copy = remote(self.held.at[n], self.landed.at[n], self.send.at[n], self.recv.at[n], device)
            copy.start()
            copy.wait()
            self.held[n + 1] = self.held[n] + self.landed[n]
        copies = [
            remote(self.held.at[3], self.four.at[pc.t], self.send.at[2 + k], self.recv.at[2 + k], pc.p_z(k))
            for k in (1, 2, 3)
        ]
        for copy in copies:
            copy.start()
        self.four[pc.t] = self.held[3]
        for k in (1, 2, 3):
            remote(
                self.held.at[3], self.four.at[pc.z(4 - k)], self.send.at[2 + k], self.recv.at[2 + k], pc.p_z(k)
            ).wait_recv()
        for copy in copies:
            copy.wait_send()


def by_rows(total, size, step, carry=()):
    def one(i, carry):
        return step(pl.ds(pl.multiple_of(i * size, size), size), carry)

    return lax.fori_loop(0, total // size, one, carry)


def fold(values):
    rows, cols = values.shape
    return jnp.sum(values.reshape(rows // 8, 8, cols), axis=0)


def line_of(folded):
    return jnp.sum(folded, axis=0, keepdims=True)


def block_kernel(
    clip_in, scales_in, seg, proj_bias, down_bias, gain, shift, qv_bias, up_bias,
    qkv_hbm, proj_hbm, up_hbm, down_hbm, tok_hbm, tea_hbm,
    bo_out, ig_out, terms_out, sums_out,
    w, l_core, l_two, l_one, l_z, lat, qkv_lat, proj_lat, scale_rows, vecs, seg_col, tok, tea, bias, act1, turned,
    turned1, qkv, probs, inv_sum, ctx, act2, normed1, inv1,
    act3, act4, fac_a, fac_b, acc, tmp, g2, g2low, dctx, held, landed, four,
    ag_send, ag_recv, rs_send, rs_recv, bias_send, bias_recv, line_send, line_recv, sum_send, sum_recv,
    credit, local,
):
    pc = Place()
    rows, model = tok.shape
    groups = 4
    cols = model // 4
    heads = cols // HEAD_DIM
    factor = HEAD_DIM ** (-0.5)
    entry = pltpu.get_barrier_semaphore()
    for device in (pc.p_core, pc.p_x, pc.p_y, pc.p_z(1), pc.p_z(2), pc.p_z(3)):
        pl.semaphore_signal(entry, inc=1, device_id=device, device_id_type=MESH)
    own_rows = pl.ds(pl.multiple_of(pc.t * rows, rows), rows)
    loads = [
        pltpu.make_async_copy(src, dst, local.at[n])
        for n, (src, dst) in enumerate(
            (
                (qkv_hbm, qkv_lat),
                (proj_hbm, proj_lat),
                (up_hbm, lat.at[:, 1]),
                (down_hbm, lat.at[:, 2]),
                (tok_hbm.at[own_rows], tok),
                (tea_hbm.at[own_rows], tea),
            )
        )
    ]
    for copy in loads:
        copy.start()
    score = tmp.at[:, pl.ds(0, rows)]
    clip = [clip_in[n] for n in range(4)]
    clip = clip + [1.0 / value for value in clip]
    lane = lax.broadcasted_iota(jnp.int32, (1, model), 1)
    for half in (0, 1):
        mixed = jnp.where(
            lane < cols,
            scales_in[half, 3],
            jnp.where(
                lane < 2 * cols,
                scales_in[half, 0],
                jnp.where(lane < 3 * cols, scales_in[half, 1], scales_in[half, 2]),
            ),
        )
        scale_rows[half : half + 1] = mixed
        scale_rows[2 + half : 3 + half] = jnp.full((1, model), scales_in[half, 4])
        scale_rows[4 + half : 5 + half] = jnp.full((1, model), scales_in[half, 5])
    vecs[0:1] = proj_bias[...].reshape(1, model)
    vecs[1:2] = down_bias[...].reshape(1, model)
    vecs[2:4] = gain[...]
    vecs[4:6] = shift[...]
    bias_own = bias.at[pc.t]
    bias_own[...] = jnp.zeros((8, model), F32)
    bias_own[0:1, cols : 2 * cols] = qv_bias[0:1]
    bias_own[0:1, 3 * cols :] = qv_bias[1:2]
    bias_own[1:2] = up_bias[...].reshape(1, model)
    seg_row = seg[pl.ds(pc.t, 1)].astype(F32)
    seg_col[...] = jnp.broadcast_to(seg_row, (128, rows)).T
    gather = Gather(w, ag_send, ag_recv, pc)
    scatter = Scatter(w, l_core, l_two, l_one, l_z, rs_send, rs_recv, credit, pc)

    def sign_of(values):
        return jnp.where(values > 0, 1.0, jnp.where(values < 0, -1.0, 0.0))

    for n in range(4):
        loads[n].wait()
    for half in (0, 1):
        for m in range(3):
            lat[half, 0, :, cols * (m + 1) : cols * (m + 2)] = qkv_lat[half, m]
        lat[half, 0, :, :cols] = proj_lat[half].astype(F32).T.astype(LOW)
    for c in range(3):

        def make(at, _, c=c):
            first = sign_of(lat[0, c, at].astype(F32)) * scale_rows[pl.ds(2 * c, 1)]
            second = sign_of(lat[1, c, at].astype(F32)) * scale_rows[pl.ds(2 * c + 1, 1)]
            w[c, pc.t, pc.j, pc.core, at] = (first + second).astype(LOW)
            return ()

        by_rows(96, 32, make)
    pl.semaphore_wait(entry, 6)

    def bias_cp(k, at):
        return remote(bias.at[at], bias.at[at], bias_send.at[k - 1], bias_recv.at[k - 1], pc.p_z(k))

    for k in (1, 2, 3):
        bias_cp(k, pc.t).start()
    for c in range(3):
        gather.z_start(c)

    loads[4].wait()

    def clip_zero(at, _):
        act1[at] = (clip[0] * jnp.tanh(tok[at].astype(F32) * clip[4])).astype(LOW)
        return ()

    by_rows(rows, 64, clip_zero)
    acc[...] = jnp.zeros_like(acc)
    loads[5].wait()
    for k in (1, 2, 3):
        bias_cp(k, pc.z(4 - k)).wait_recv()
    for c in range(3):
        gather.z_wait_xy_start(c)
        if c == 0:
            gather.relay(0)
    gather.finish(0)

    def weight(c, g):
        return w[c, g].reshape(model, model)

    def attention(g, _):
        tmp[...] = dot_nn(act1[...], weight(0, g))
        mult = jnp.where(lax.broadcasted_iota(jnp.int32, (1, model), 1) < 2 * cols, factor, 1.0)

        def low(at, _):
            qkv[g, at] = ((tmp[at] + bias[g, 0:1]) * mult).astype(LOW)
            return ()

        by_rows(rows, 64, low)
        for h in range(heads):
            q = qkv[g, :, cols + HEAD_DIM * h : cols + HEAD_DIM * (h + 1)]
            k = qkv[g, :, 2 * cols + HEAD_DIM * h : 2 * cols + HEAD_DIM * (h + 1)]
            v = qkv[g, :, 3 * cols + HEAD_DIM * h : 3 * cols + HEAD_DIM * (h + 1)]
            score[...] = dot_nt(k, q)
            for b in range(rows // 128):
                lanes = slice(128 * b, 128 * (b + 1))
                values = jnp.where(seg_col[...] == seg_row[:, lanes], score[:, lanes], NO_MATCH)
                terms = jnp.exp(values - jnp.max(values, axis=0, keepdims=True))
                probs[heads * g + h, :, lanes] = terms.astype(LOW)
                inv_sum[g, h : h + 1, lanes] = 1.0 / jnp.sum(terms, axis=0, keepdims=True)
            at = slice(HEAD_DIM * h, HEAD_DIM * (h + 1))
            ctx[g, at] = dot_tn(v, probs[heads * g + h]) * inv_sum[g, h : h + 1]
        act2[g] = (clip[1] * jnp.tanh(ctx[g] * clip[5])).astype(LOW)
        acc[...] += dot_tt(act2[g], weight(0, g)[:, :cols]).astype(LOW).astype(F32)
        return 0

    lax.fori_loop(0, 2, attention, 0)
    gather.relay(1)
    lax.fori_loop(2, groups, attention, 0)
    gather.relay(2)

    def norm_one(at, _):
        values = tok[at].astype(F32) + (acc[at] + vecs[0:1])
        centre = values - jnp.mean(values, axis=-1, keepdims=True)
        scale_inv = lax.rsqrt(jnp.mean(centre * centre, axis=-1, keepdims=True) + 1e-12)
        normed = centre * scale_inv
        normed1[at] = normed
        inv1[at] = scale_inv
        act3[at] = (clip[2] * jnp.tanh((normed * vecs[2:3] + vecs[4:5]) * clip[6])).astype(LOW)
        return ()

    by_rows(rows, 64, norm_one)
    acc[...] = jnp.zeros_like(acc)
    gather.finish(1)

    def up(g, _):
        tmp[...] = dot_nn(act3[...], weight(1, g))

        def act(at, _):
            hidden = tmp[at] + bias[g, 1:2]
            cdf = 0.5 * (1.0 + lax.erf(hidden * (0.5**0.5)))
            pdf = jnp.exp(-0.5 * hidden * hidden) * 0.3989422804014327
            ratio = (hidden * cdf) * clip[7]
            bent = jnp.tanh(ratio)
            slope = 1.0 - bent * bent
            act4[g, at] = (clip[3] * bent).astype(LOW)
            fac_a[g, at] = (slope * (cdf + hidden * pdf)).astype(LOW)
            fac_b[g, at] = (bent - ratio * slope).astype(LOW)
            return ()

        by_rows(rows, 32, act)
        return 0

    lax.fori_loop(0, groups, up, 0)
    gather.finish(2)

    def down(g, _):
        acc[...] += dot_nt(act4[g], weight(2, g)).astype(LOW).astype(F32)
        return 0

    lax.fori_loop(0, groups, down, 0)

    zero = jnp.zeros((8, model), F32)

    def norm_two(at, carry):
        gain_sum, shift_sum, bias_sum = carry
        values = (normed1[at] * vecs[2:3] + vecs[4:5]) + (acc[at] + vecs[1:2])
        centre = values - jnp.mean(values, axis=-1, keepdims=True)
        scale_inv = lax.rsqrt(jnp.mean(centre * centre, axis=-1, keepdims=True) + 1e-12)
        normed = centre * scale_inv
        y = normed * vecs[3:4] + vecs[5:6]
        grad = y - tea[at].astype(F32)
        tea[at] = y.astype(LOW)
        scaled = grad * vecs[3:4]
        grad_in = scale_inv * (
            scaled
            - jnp.mean(scaled, axis=-1, keepdims=True)
            - normed * jnp.mean(scaled * normed, axis=-1, keepdims=True)
        )
        g2[at] = grad_in
        g2low[at] = grad_in.astype(LOW)
        return (gain_sum + fold(grad * normed), shift_sum + fold(grad), bias_sum + fold(grad_in))

    gain_sum, shift_sum, bias_sum = by_rows(rows, 64, norm_two, (zero, zero, zero))
    held[0, 11:12] = line_of(gain_sum)
    held[0, 13:14] = line_of(shift_sum)
    held[0, 9:10] = line_of(bias_sum)
    for c in range(3):
        gather.sent(c)
    bo = Line(tea, bo_out, line_send.at[0], line_recv.at[0], local.at[6], pc)
    bo.start()

    turned[...] = g2low[...].T

    def ffn_back_one(g, total):
        tmp[...] = dot_nn(g2low[...], weight(2, g))
        w[2, g] = dot_nn(turned[...], act4[g]).astype(LOW).reshape(w.shape[2:])

        def back(at, carry):
            clip_sum, bias_sum = carry
            grad = tmp[at]
            low = (grad * fac_a[g, at].astype(F32)).astype(LOW)
            clip_sum = clip_sum + fold(grad * fac_b[g, at].astype(F32))
            fac_a[g, at] = low
            return (clip_sum, bias_sum + fold(low.astype(F32)))

        total, bias_sum = by_rows(rows, 64, back, (total, zero))
        held[0, pl.ds(4 + g, 1)] = line_of(bias_sum)
        return total

    clip_sum = lax.fori_loop(0, groups, ffn_back_one, zero)
    held[0, 17:18] = line_of(clip_sum)
    scatter.core_start(2)
    turned[...] = act3[...].T
    acc[...] = jnp.zeros_like(acc)

    def ffn_back_two(g, _):
        acc[...] += dot_nt(fac_a[g], weight(1, g)).astype(LOW).astype(F32)
        w[1, g] = dot_nn(turned[...], fac_a[g]).astype(LOW).reshape(w.shape[2:])
        return 0

    lax.fori_loop(0, 2, ffn_back_two, 0)
    scatter.core_fin(2)
    lax.fori_loop(2, groups, ffn_back_two, 0)
    scatter.core_start(1)

    def norm_one_back(at, carry):
        clip_sum, gain_sum, shift_sum, bias_sum = carry
        normed = normed1[at]
        ratio = (normed * vecs[2:3] + vecs[4:5]) * clip[6]
        bent = jnp.tanh(ratio)
        slope = 1.0 - bent * bent
        grad_three = acc[at]
        grad = g2[at] + grad_three * slope
        scaled = grad * vecs[2:3]
        grad_in = inv1[at] * (
            scaled
            - jnp.mean(scaled, axis=-1, keepdims=True)
            - normed * jnp.mean(scaled * normed, axis=-1, keepdims=True)
        )
        g2[at] = grad_in
        g2low[at] = grad_in.astype(LOW)
        return (
            clip_sum + fold(grad_three * (bent - ratio * slope)),
            gain_sum + fold(grad * normed),
            shift_sum + fold(grad),
            bias_sum + fold(grad_in),
        )

    clip_sum, gain_sum, shift_sum, bias_sum = by_rows(rows, 64, norm_one_back, (zero, zero, zero, zero))
    held[0, 16:17] = line_of(clip_sum)
    held[0, 10:11] = line_of(gain_sum)
    held[0, 12:13] = line_of(shift_sum)
    held[0, 8:9] = line_of(bias_sum)
    acc[...] = jnp.zeros_like(acc)
    dqkv = act4.at[0]
    dscore = fac_b.at[0, :, pl.ds(0, rows)]
    dqkv[...] = jnp.zeros_like(dqkv)
    turned1[...] = act1[...].T
    scatter.two_fin(2)
    bo.step(1)
    scatter.core_fin(1)
    small_zero = jnp.zeros((8, rows), F32)
    turned[...] = g2low[...].T

    def attention_back(g, total):
        w_g = weight(0, g)
        grad = dot_tn(w_g[:, :cols], turned[...])
        g_proj = dot_nt(turned[...], act2[g]).astype(LOW)
        ratio = ctx[g] * clip[5]
        bent = jnp.tanh(ratio)
        slope = 1.0 - bent * bent
        total = total + fold(grad * (bent - ratio * slope))
        grad = grad * slope
        for h in range(heads):
            at = slice(HEAD_DIM * h, HEAD_DIM * (h + 1))
            q_at = slice(cols + HEAD_DIM * h, cols + HEAD_DIM * (h + 1))
            k_at = slice(2 * cols + HEAD_DIM * h, 2 * cols + HEAD_DIM * (h + 1))
            v_at = slice(3 * cols + HEAD_DIM * h, 3 * cols + HEAD_DIM * (h + 1))
            scaled = grad[at] * inv_sum[g, h : h + 1]
            dctx[at] = scaled.astype(LOW)
            mean = jnp.sum(scaled * ctx[g, at], axis=0, keepdims=True)
            score[...] = dot_nn(qkv[g, :, v_at], dctx[at])
            for b in range(4):
                some = slice(rows // 4 * b, rows // 4 * (b + 1))
                dscore[some] = (probs[heads * g + h, some].astype(F32) * (score[some] - mean)).astype(LOW)
            dqkv[:, k_at] = dot_nn(dscore[...], qkv[g, :, q_at]).astype(LOW)
            dqkv[:, v_at] = dot_nt(probs[heads * g + h], dctx[at]).astype(LOW)
            dqkv[:, q_at] = (dot_tn(qkv[g, :, k_at], dscore[...]) * factor).T.astype(LOW)

        def sums(at, carry):
            return carry + fold(dqkv[at].astype(F32))

        held[0, pl.ds(g, 1)] = line_of(by_rows(rows, 64, sums, zero))
        acc[...] += dot_nt(dqkv[...], w_g).astype(LOW).astype(F32)
        w[0, g] = dot_nn(turned1[...], dqkv[...]).astype(LOW).reshape(w.shape[2:])
        w[0, g, :, :, :, :cols] = g_proj.reshape(w.shape[2:5] + (cols,))
        return total

    clip_sum = lax.fori_loop(0, 1, attention_back, small_zero)
    scatter.one_fin(2)
    clip_sum = lax.fori_loop(1, 2, attention_back, clip_sum)
    scatter.two_fin(1)
    bo.step(2)
    clip_sum = lax.fori_loop(2, 3, attention_back, clip_sum)
    scatter.one_fin(1)
    clip_sum = lax.fori_loop(3, 4, attention_back, clip_sum)
    held[0, 15:16, :rows] = line_of(clip_sum)
    held[0, 15:16, rows:] = jnp.zeros((1, model - rows), F32)
    scatter.core_start(0)

    def clip_zero_back(at, clip_sum):
        ratio = tok[at].astype(F32) * clip[4]
        bent = jnp.tanh(ratio)
        slope = 1.0 - bent * bent
        grad = acc[at]
        act3[at] = (g2[at] + grad * slope).astype(LOW)
        return clip_sum + fold(grad * (bent - ratio * slope))

    held[0, 14:15] = line_of(by_rows(rows, 64, clip_zero_back, zero))
    ig = Line(act3, ig_out, line_send.at[1], line_recv.at[1], local.at[7], pc)
    bo.step(3)
    ig.start()
    scatter.core_fin(0)

    def finish(c):
        def one(at, carry):
            first, second = carry
            grad = w[c, pc.t, pc.j, pc.core, at].astype(F32)
            for k in range(3):
                grad = grad + l_z[c, k, at].astype(F32)
            out = []
            for half, carried in ((0, first), (1, second)):
                latent = lat[half, c, at].astype(F32)
                scale = scale_rows[pl.ds(2 * c + half, 1)]
                terms_out[half, c, at] = jnp.where(jnp.abs(latent) < 1.0, grad * scale, 0.0)
                out.append(carried + fold(grad * sign_of(latent)))
            return tuple(out)

        scatter.z_wait(c)
        first, second = by_rows(96, 32, one, (zero, zero))
        held[0, 18 + 2 * c : 19 + 2 * c] = line_of(first)
        held[0, 19 + 2 * c : 20 + 2 * c] = line_of(second)

    finish(2)
    scatter.two_fin(0)
    ig.step(1)
    scatter.one_fin(0)
    finish(1)
    finish(0)
    ig.step(2)
    sums = SmallSum(held, landed, four, sum_send, sum_recv, pc)
    sums.run()
    sums_out[...] = (four[0] + four[1]) + (four[2] + four[3])
    ig.step(3)
    for k in (1, 2, 3):
        bias_cp(k, pc.t).wait_send()
    for c in range(3):
        scatter.sent(c)
    bo.sent()
    ig.sent()


def finish_kernel(
    bo_in, ig_in, terms, sums,
    bo_out, ig_out, qkv, qv_bias, proj, proj_bias, up, up_bias, down, down_bias, gain, shift, clip, scale,
    bo_held, ig_held, ig_wide, sems,
):
    parts, rows, model = bo_in.shape
    cols = model // 4
    t = lax.axis_index("tensor")

    def bo_get(n):
        return pltpu.make_async_copy(bo_in.at[n], bo_held.at[n], sems.at[0, n])

    def bo_put(n):
        return pltpu.make_async_copy(bo_held.at[n], bo_out.at[pl.ds(n * rows, rows)], sems.at[1, n])

    def ig_get(n):
        return pltpu.make_async_copy(ig_in.at[n], ig_held.at[n], sems.at[2, n])

    def ig_put(n):
        return pltpu.make_async_copy(ig_wide.at[n], ig_out.at[pl.ds(n * rows, rows)], sems.at[3, n])

    for n in range(parts):
        ig_get(n).start()
    for n in range(parts):
        bo_get(n).start()
    for n in range(parts):
        ig_get(n).wait()

        def widen(at, _, n=n):
            ig_wide[n, at] = ig_held[n, at].astype(F32)
            return ()

        by_rows(rows, 64, widen)
        ig_put(n).start()
    for n in range(parts):
        bo_get(n).wait()
        bo_put(n).start()
    for half in (0, 1):
        for m in range(3):
            qkv[half, m] = terms[half, 0, :, cols * (m + 1) : cols * (m + 2)]
        proj[half] = terms[half, 0, :, :cols].T
        up[half] = terms[half, 1]
        down[half] = terms[half, 2]
    own = sums[pl.ds(t, 1)]
    qv_bias[0:1] = own[:, cols : 2 * cols]
    qv_bias[1:2] = own[:, 3 * cols :]
    up_bias[...] = sums[pl.ds(4 + t, 1)].reshape(model)
    proj_bias[...] = sums[8:9].reshape(model)
    down_bias[...] = sums[9:10].reshape(model)
    gain[...] = sums[10:12]
    shift[...] = sums[12:14]
    for n in range(4):
        clip[n] = jnp.sum(sums[14 + n : 15 + n])
    for half in (0, 1):
        for m, at in enumerate((1, 2, 3, 0)):
            scale[half, m] = jnp.sum(sums[18 + half : 19 + half, cols * at : cols * (at + 1)])
        for m in (4, 5):
            scale[half, m] = jnp.sum(sums[12 + 2 * m + half : 13 + 2 * m + half])
    for n in range(parts):
        ig_put(n).wait()
        bo_put(n).wait()


def block(clip, scales, seg, proj_bias, down_bias, gain, shift, qv_bias, up_bias, qkv, proj, up, down, tokens, teacher):
    rows = seg.shape[1]
    model = tokens.shape[1]
    cols = model // 4
    vm = pltpu.VMEM
    dma = pltpu.SemaphoreType.DMA
    whole = pl.BlockSpec(memory_space=pltpu.VMEM)
    small = pl.BlockSpec(memory_space=pltpu.SMEM)
    away = pl.BlockSpec(memory_space=pl.ANY)
    own = up.shape[1]
    bo, ig, terms, sums = pl.pallas_call(
        block_kernel,
        out_shape=(
            jax.ShapeDtypeStruct((4, rows, model), LOW),
            jax.ShapeDtypeStruct((4, rows, model), LOW),
            jax.ShapeDtypeStruct((2, 3, own, model), F32),
            jax.ShapeDtypeStruct((24, model), F32),
        ),
        in_specs=[small] * 2 + [whole] * 7 + [away] * 6,
        out_specs=(away, away, whole, whole),
        scratch_shapes=[
            vm((3, 4, 4, 2, own, model), LOW),
            vm((2, 4, 4, own, model), LOW),
            vm((3, 2, 2, 2, own, model), LOW),
            vm((3, 2, 2, own, model), LOW),
            vm((3, 3, own, model), LOW),
            vm((2, 3, own, model), LOW),
            vm(qkv.shape, LOW),
            vm(proj.shape, LOW),
            vm((8, model), F32),
            vm((8, model), F32),
            vm((rows, 128), F32),
            vm((rows, model), LOW),
            vm((rows, model), LOW),
            vm((4, 8, model), F32),
            vm((rows, model), LOW),
            vm((model, rows), LOW),
            vm((model, rows), LOW),
            vm((4, rows, model), LOW),
            vm((model // HEAD_DIM, rows, rows), LOW),
            vm((4, 8, rows), F32),
            vm((4, cols, rows), F32),
            vm((4, cols, rows), LOW),
            vm((rows, model), F32),
            vm((rows, 1), F32),
            vm((rows, model), LOW),
            vm((4, rows, model), LOW),
            vm((4, rows, model), LOW),
            vm((4, rows, model), LOW),
            vm((rows, model), F32),
            vm((rows, model), F32),
            vm((rows, model), F32),
            vm((rows, model), LOW),
            vm((cols, rows), LOW),
            vm((4, 24, model), F32),
            vm((3, 24, model), F32),
            vm((4, 24, model), F32),
            dma((3, 17)), dma((3, 17)), dma((3, 11)), dma((3, 11)), dma((3,)), dma((3,)),
            dma((2, 2, 3)), dma((2, 2, 3)), dma((6,)), dma((6,)),
            pltpu.SemaphoreType.REGULAR,
            dma((8,)),
        ],
        compiler_params=pltpu.CompilerParams(
            collective_id=0, has_side_effects=True, vmem_limit_bytes=67043328
        ),
    )(clip, scales, seg, proj_bias, down_bias, gain, shift, qv_bias, up_bias, qkv, proj, up, down, tokens, teacher)
    f32 = lambda *shape: jax.ShapeDtypeStruct(shape, F32)
    return pl.pallas_call(
        finish_kernel,
        out_shape=(
            jax.ShapeDtypeStruct((4 * rows, model), LOW),
            f32(4 * rows, model),
            f32(2, 3, own, cols),
            f32(2, cols),
            f32(2, cols, own),
            f32(model),
            f32(2, own, model),
            f32(model),
            f32(2, own, model),
            f32(model),
            f32(2, model),
            f32(2, model),
            f32(4),
            f32(2, 6),
        ),
        in_specs=[away, away, whole, whole],
        out_specs=(away, away) + (whole,) * 10 + (small, small),
        scratch_shapes=[
            vm((4, rows, model), LOW),
            vm((4, rows, model), LOW),
            vm((4, rows, model), F32),
            dma((4, 4)),
        ],
        compiler_params=pltpu.CompilerParams(vmem_limit_bytes=67043328),
    )(bo, ig, terms, sums)


def squash(values, clip_at):
    ratio = values / clip_at
    bent = jnp.tanh(ratio)
    return (clip_at * bent, bent, ratio)


def squash_back(gradient, bent, ratio):
    slope = 1.0 - bent * bent
    return (gradient * slope, jnp.sum(gradient * (bent - ratio * slope)))


def norm_parts(values, gain, shift):
    centre = values - jnp.mean(values, axis=-1, keepdims=True)
    scale_inv = lax.rsqrt(jnp.mean(centre * centre, axis=-1, keepdims=True) + 1e-12)
    normed = centre * scale_inv
    return (normed * gain + shift, normed, scale_inv)


def norm_back(gradient, normed, scale_inv, gain):
    scaled = gradient * gain
    return scale_inv * (
        scaled
        - jnp.mean(scaled, axis=-1, keepdims=True)
        - normed * jnp.mean(scaled * normed, axis=-1, keepdims=True)
    )


def exact_gelu(values):
    return jax.nn.gelu(values, approximate=False)


def plain_shards(
    tokens,
    teacher,
    segment_ids,
    qkv_latent,
    qv_bias,
    proj_latent,
    proj_bias,
    up_latent,
    up_bias,
    down_latent,
    down_bias,
    norm_gain,
    norm_shift,
    clip_bounds,
    binary_scales,
):
    groups = lax.axis_size("tensor")
    parts = lax.axis_size("dp")
    group = lax.axis_index("tensor")
    seqs = segment_ids.shape[0] // groups
    length = segment_ids.shape[1]
    rows = seqs * length
    model = tokens.shape[1]
    own_rows = qkv_latent.shape[1]
    head_cols = qkv_latent.shape[3]
    units = up_latent.shape[2]
    heads = head_cols // HEAD_DIM

    tokens = lax.dynamic_slice_in_dim(tokens, group * rows, rows, 0)
    teacher = lax.dynamic_slice_in_dim(teacher, group * rows, rows, 0)
    segment_ids = lax.dynamic_slice_in_dim(segment_ids, group * seqs, seqs, 0)

    latents = jnp.concatenate(
        [
            qkv_latent.reshape(2, own_rows, 3 * head_cols),
            proj_latent.transpose(0, 2, 1),
            up_latent,
            down_latent.transpose(0, 2, 1),
        ],
        axis=2,
    )
    widths = [head_cols] * 4 + [units] * 2
    scale_cols = jnp.concatenate(
        [jnp.broadcast_to(binary_scales[m][:, None], (2, w)) for m, w in enumerate(widths)], axis=1
    )
    signs = jnp.sign(latents).astype(F32)
    w_own = (scale_cols[0] * signs[0] + scale_cols[1] * signs[1]).astype(LOW)
    w_all = lax.all_gather(w_own, ("tensor", "dp"), axis=0, tiled=False)
    w_all = w_all.reshape(groups, model, 4 * head_cols + 2 * units)
    bias_all = lax.all_gather(
        jnp.concatenate([qv_bias[0], qv_bias[1], up_bias]), "tensor", axis=0, tiled=False
    )
    edge = 3 * head_cols

    inputs = tokens.astype(F32)
    act_one_full, bent_zero, ratio_zero = squash(inputs, clip_bounds[0])
    act_one = act_one_full.astype(LOW)
    same_doc = (segment_ids[:, :, None] == segment_ids[:, None, :])[:, None]
    factor = HEAD_DIM ** (-0.5)

    attention = jnp.zeros((rows, model), F32)
    kept = []
    for g in range(groups):
        w_qkv = w_all[g, :, :edge]
        bias = jnp.concatenate(
            [
                bias_all[g, :head_cols],
                jnp.zeros((head_cols,), F32),
                bias_all[g, head_cols : 2 * head_cols],
            ]
        )
        qkv = (dot_nn(act_one, w_qkv) + bias).astype(LOW).reshape(seqs, length, 3, heads, HEAD_DIM)
        q, k, v = qkv[:, :, 0], qkv[:, :, 1], qkv[:, :, 2]
        scores = jnp.einsum("nqhe,nkhe->nhqk", q, k, preferred_element_type=F32) * factor
        scores = jnp.where(same_doc, scores, -1000000000.0)
        top = jnp.max(scores, axis=-1, keepdims=True)
        terms = jnp.exp(scores - top)
        total = jnp.sum(terms, axis=-1, keepdims=True)
        probs = (terms / total).astype(LOW)
        context = jnp.einsum("nhqk,nkhe->nqhe", probs, v, preferred_element_type=F32).reshape(
            rows, head_cols
        )
        act_full, bent_one, ratio_one = squash(context, clip_bounds[1])
        act_two = act_full.astype(LOW)
        attention += dot_nt(act_two, w_all[g, :, edge : edge + head_cols]).astype(LOW).astype(F32)
        kept.append((q, k, v, probs, act_two, bent_one, ratio_one))
    h_one, normed_one, inv_one = norm_parts(inputs + (attention + proj_bias), norm_gain[0], norm_shift[0])
    act_three_full, bent_two, ratio_two = squash(h_one, clip_bounds[2])
    act_three = act_three_full.astype(LOW)

    feed = jnp.zeros((rows, model), F32)
    start_up = 4 * head_cols
    start_down = start_up + units
    kept_ffn = []
    for g in range(groups):
        hidden = dot_nn(act_three, w_all[g, :, start_up:start_down]) + bias_all[g, 2 * head_cols :]
        activated, gelu_back = jax.vjp(exact_gelu, hidden)
        act_full, bent_three, ratio_three = squash(activated, clip_bounds[3])
        act_four = act_full.astype(LOW)
        feed += dot_nt(act_four, w_all[g, :, start_down:]).astype(LOW).astype(F32)
        kept_ffn.append((act_four, gelu_back, bent_three, ratio_three))
    y_full, normed_two, inv_two = norm_parts(h_one + (feed + down_bias), norm_gain[1], norm_shift[1])
    block_out = lax.all_gather(y_full.astype(LOW), "tensor", axis=0, tiled=True)

    out_grad = y_full - teacher.astype(F32)
    gain_two = jnp.sum(out_grad * normed_two, axis=0)
    shift_two = jnp.sum(out_grad, axis=0)
    grad_two = norm_back(out_grad, normed_two, inv_two, norm_gain[1])
    down_bias_part = jnp.sum(grad_two, axis=0)
    grad_two_low = grad_two.astype(LOW)
    grads = [[] for _ in range(groups)]
    up_bias_part = []
    clip_three = 0.0
    grad_three = jnp.zeros((rows, model), F32)
    g_down, g_up = [], []
    for g in range(groups):
        act_four, gelu_back, bent_three, ratio_three = kept_ffn[g]
        g_down.append(dot_tn(grad_two_low, act_four).astype(LOW))
        grad_four = dot_nn(grad_two_low, w_all[g, :, start_down:])
        grad_act, clip_part = squash_back(grad_four, bent_three, ratio_three)
        clip_three += clip_part
        grad_hidden = gelu_back(grad_act)[0].astype(LOW)
        up_bias_part.append(jnp.sum(grad_hidden.astype(F32), axis=0))
        g_up.append(dot_tn(act_three, grad_hidden).astype(LOW))
        grad_three += dot_nt(grad_hidden, w_all[g, :, start_up:start_down]).astype(LOW).astype(F32)
    grad_three_in, clip_two = squash_back(grad_three, bent_two, ratio_two)
    grad_h = grad_two + grad_three_in
    gain_one = jnp.sum(grad_h * normed_one, axis=0)
    shift_one = jnp.sum(grad_h, axis=0)
    grad_one = norm_back(grad_h, normed_one, inv_one, norm_gain[0])
    proj_bias_part = jnp.sum(grad_one, axis=0)
    grad_one_low = grad_one.astype(LOW)

    clip_one = 0.0
    grad_act_one = jnp.zeros((rows, model), F32)
    g_att = []
    q_bias_part, v_bias_part = [], []
    for g in range(groups):
        q, k, v, probs, act_two, bent_one, ratio_one = kept[g]
        w_o = w_all[g, :, edge : edge + head_cols]
        g_proj = dot_tn(grad_one_low, act_two).astype(LOW)
        grad_ctx, clip_part = squash_back(dot_nn(grad_one_low, w_o), bent_one, ratio_one)
        clip_one += clip_part
        grad_ctx = grad_ctx.astype(LOW).reshape(seqs, length, heads, HEAD_DIM)
        grad_v = jnp.einsum("nhqk,nqhe->nkhe", probs, grad_ctx, preferred_element_type=F32)
        grad_probs = jnp.einsum("nqhe,nkhe->nhqk", grad_ctx, v, preferred_element_type=F32)
        probs_wide = probs.astype(F32)
        grad_scores = (
            probs_wide * (grad_probs - jnp.sum(probs_wide * grad_probs, axis=-1, keepdims=True))
        ).astype(LOW)
        grad_q = jnp.einsum("nhqk,nkhe->nqhe", grad_scores, k, preferred_element_type=F32) * factor
        grad_k = jnp.einsum("nhqk,nqhe->nkhe", grad_scores, q, preferred_element_type=F32) * factor
        grad_qkv = jnp.stack([grad_q, grad_k, grad_v], axis=2).astype(LOW).reshape(rows, edge)
        sums = jnp.sum(grad_qkv.astype(F32), axis=0)
        q_bias_part.append(sums[:head_cols])
        v_bias_part.append(sums[2 * head_cols :])
        g_qkv = dot_tn(act_one, grad_qkv).astype(LOW)
        g_att.append(jnp.concatenate([g_qkv, g_proj], axis=1))
        grad_act_one += dot_nt(grad_qkv, w_all[g, :, :edge]).astype(LOW).astype(F32)
    grad_inputs, clip_zero = squash_back(grad_act_one, bent_zero, ratio_zero)
    input_grad = lax.all_gather(
        (grad_one + grad_inputs).astype(LOW), "tensor", axis=0, tiled=True
    ).astype(F32)

    g_all = jnp.stack(
        [jnp.concatenate([g_att[g], g_up[g], g_down[g]], axis=1) for g in range(groups)]
    ).reshape(groups * parts, own_rows, 4 * head_cols + 2 * units)
    g_own = lax.psum_scatter(
        g_all, ("tensor", "dp"), scatter_dimension=0, tiled=False
    ).astype(F32)

    keep = jnp.abs(latents) < 1.0
    terms = jnp.where(keep, g_own[None] * scale_cols[:, None], 0.0)
    col_sums = jnp.sum(g_own[None] * signs, axis=1)
    ends = [0]
    for w in widths:
        ends.append(ends[-1] + w)
    scale_parts = jnp.stack([jnp.sum(col_sums[:, a:b], axis=1) for a, b in zip(ends[:-1], ends[1:])])

    clip_parts = jnp.stack([clip_zero, clip_one, clip_two, clip_three])
    small = jnp.concatenate(
        [
            jnp.concatenate(q_bias_part),
            jnp.concatenate(v_bias_part),
            jnp.concatenate(up_bias_part),
            proj_bias_part,
            down_bias_part,
            gain_one,
            gain_two,
            shift_one,
            shift_two,
            clip_parts,
            scale_parts.reshape(-1),
        ]
    )
    small = lax.psum(small, ("dp", "tensor"))
    pos = 0

    def take(n):
        nonlocal pos
        out = small[pos : pos + n]
        pos += n
        return out

    q_bias = lax.dynamic_slice_in_dim(take(groups * head_cols), group * head_cols, head_cols, 0)
    v_bias = lax.dynamic_slice_in_dim(take(groups * head_cols), group * head_cols, head_cols, 0)
    up_bias_grad = lax.dynamic_slice_in_dim(take(groups * units), group * units, units, 0)
    proj_bias_grad = take(model)
    down_bias_grad = take(model)
    gain_grad = take(2 * model).reshape(2, model)
    shift_grad = take(2 * model).reshape(2, model)
    clip_grad = take(4)
    scale_grad = take(12).reshape(6, 2)
    return (
        block_out,
        input_grad,
        terms[:, :, :edge].reshape(2, own_rows, 3, head_cols),
        jnp.stack([q_bias, v_bias]),
        terms[:, :, edge : edge + head_cols].transpose(0, 2, 1),
        proj_bias_grad,
        terms[:, :, start_up:start_down],
        up_bias_grad,
        terms[:, :, start_down:].transpose(0, 2, 1),
        down_bias_grad,
        gain_grad,
        shift_grad,
        clip_grad,
        scale_grad,
    )


def fits(mesh):
    return mesh.shape["dp"] == 8 and mesh.shape["tensor"] == 4


def fused_shards(
    tokens,
    teacher,
    segment_ids,
    qkv_latent,
    qv_bias,
    proj_latent,
    proj_bias,
    up_latent,
    up_bias,
    down_latent,
    down_bias,
    norm_gain,
    norm_shift,
    clip_bounds,
    binary_scales,
):
    outs = block(
        clip_bounds,
        binary_scales.T,
        segment_ids,
        proj_bias,
        down_bias,
        norm_gain,
        norm_shift,
        qv_bias,
        up_bias,
        qkv_latent.transpose(0, 2, 1, 3),
        proj_latent,
        up_latent,
        down_latent.transpose(0, 2, 1),
        tokens,
        teacher,
    )
    outs = list(outs)
    outs[2] = outs[2].transpose(0, 2, 1, 3)
    outs[8] = outs[8].transpose(0, 2, 1)
    outs[13] = outs[13].T
    return tuple(outs)


def solution(mesh):
    return jax.shard_map(
        fused_shards if fits(mesh) else plain_shards,
        mesh=mesh,
        in_specs=(
            P("dp", None),
            P("dp", None),
            P("dp", None),
            P(None, "dp", None, "tensor"),
            P(None, "tensor"),
            P(None, "tensor", "dp"),
            P(),
            P(None, "dp", "tensor"),
            P("tensor"),
            P(None, "tensor", "dp"),
            P(),
            P(),
            P(),
            P(),
            P(),
        ),
        out_specs=(
            P("dp", None),
            P("dp", None),
            P(None, "dp", None, "tensor"),
            P(None, "tensor"),
            P(None, "tensor", "dp"),
            P(),
            P(None, "dp", "tensor"),
            P("tensor"),
            P(None, "tensor", "dp"),
            P(),
            P(),
            P(),
            P(),
            P(),
        ),
        check_vma=False,
    )
```
